32 devices in a mesh: parts: 2 (over y), dp: 4 (over z), filt: 4 (over x, core).
Axes of the slice: x: 2, y: 2, z: 4, core: 2. Of those that a mesh axis runs over, the one named last changes fastest.
Arguments:
- inputs: bfloat16 [1008, 8, 576], P('filt', ('parts', 'dp')), parts along dimension 1, may hold values from -6 to 6
- filters: bfloat16 [128, 9, 63, 252], P(('parts', 'dp'), None, None, 'filt'), parts along dimension 0, may hold values from -0.0625 to 0.0625
- out_grad: bfloat16 [1008, 8, 576], P('filt', ('parts', 'dp')), parts along dimension 1, may hold values from -6 to 6
- block_owner: int32 [128], P('parts'), parts along dimension 0, may hold values from 0 to 63, each once
Outputs:
- conv_out: bfloat16 [1008, 8, 576], P('filt', ('parts', 'dp')), parts along dimension 1
- in_grad: bfloat16 [1008, 8, 576], P('filt', ('parts', 'dp')), parts along dimension 1
The draws below stay inside these ranges and needn't reach their ends.
There are 2 independent parts, one for each index of `parts`. The reference program is written for one: setup_inputs(seed, part) draws one part's arguments, and reference() takes and returns one part's arrays. A program takes and returns all parts, laid end to end along the dimension named above; each array names one. Nothing has to cross between parts.
Inputs may be any that keep to these rules, and one draw needn't show every extreme that they name: `block_owner`: each slot holds exactly one block; slots are split evenly and in order along dp.
All inputs are finite; a program needn't handle non-finite values.
Results may differ from the reference program's by a relative error of at most 0.001.
Values may be sent and summed in bfloat16 or wider, within the bound.
A program may use at most 64 MiB of HBM per device.

```python
import jax
import jax.numpy as jnp

GW = 1008
HH = 24
WW = 24
CO_SPLIT = 4
CI_SPLIT = 16
IMAGES = 4
PIX = 576
COB = 63
CIB = 63
NBLK = 64
N_FILT = 4


def levels(rng, shape, cuts, low, top_value):
    def one(axis_at, blocks):
        heights = jax.random.uniform(jax.random.fold_in(jax.random.fold_in(rng, 6), axis_at), (blocks,), jnp.float32, low / len(cuts), top_value / len(cuts))
        return jnp.repeat(jnp.exp(heights), shape[axis_at] // blocks).reshape((-1,) + (1,) * (len(shape) - axis_at - 1))

    loudness = one(*cuts[0])
    for cut in cuts[1:]:
        loudness = loudness * one(*cut)
    return loudness


def noise(own_key, dims, width, limit, split=(), kind=jnp.bfloat16):
    factor_of = levels(own_key, dims, split, -0.22, 0.18) if split else 1.0
    array = jax.random.normal(own_key, dims, jnp.float32) * width * factor_of
    return jnp.minimum(jnp.maximum(array, -limit), limit).astype(kind)


def setup_inputs(seed: int = 0, part: int = 0) -> dict:
    seeds = jax.random.split(jax.random.key(seed), 5)
    part_splits = jax.random.split(jax.random.fold_in(seeds[4], part), 5)
    inputs = noise(part_splits[0], (GW, IMAGES, PIX), 1.0, 6.0, ((0, 4), (1, 4)))
    filters = noise(part_splits[1], (NBLK, 9, CIB, N_FILT * COB), (9 * GW) ** -0.5, 0.0625, ((0, 4), (3, 4)))
    out_grad = noise(part_splits[2], (GW, IMAGES, PIX), 1.0, 6.0, ((0, 4), (1, 4)))
    block_owner = jax.random.permutation(part_splits[3], NBLK).astype(jnp.int32)
    return {"inputs": inputs, "filters": filters, "out_grad": out_grad, "block_owner": block_owner}


def assemble(filters, block_owner):
    ordered = jnp.take(filters, block_owner.astype(jnp.int32), axis=0)
    ordered = ordered.reshape(CO_SPLIT, CI_SPLIT, 9, CIB, N_FILT, COB)
    return ordered.transpose(2, 1, 3, 4, 0, 5).reshape(9, GW, GW)


def tap_window(flat, shift_row, shift_col):
    padded = jnp.pad(flat, ((0, 0), (0, 0), (WW + 1, WW + 1)))
    begin = (WW + 1) + (shift_row - 1) * WW + (shift_col - 1)
    piece = padded[:, :, begin:begin + HH * WW]
    column = jnp.arange(HH * WW, dtype=jnp.int32) % WW + (shift_col - 1)
    valid = (column >= 0) & (column < WW)
    piece = jnp.where(valid[None, None, :], piece, jnp.zeros_like(piece))
    return piece.reshape(flat.shape[0], flat.shape[1] * HH * WW)


def reference(inputs, filters, out_grad, block_owner):
    weights = assemble(filters, block_owner)
    forward_sum = jnp.zeros((GW, IMAGES * PIX), jnp.float32)
    backward_sum = jnp.zeros((GW, IMAGES * PIX), jnp.float32)
    for offset in range(9):
        shift_row = offset // 3
        shift_col = offset % 3
        window = tap_window(inputs, shift_row, shift_col)
        forward_sum = forward_sum + jnp.dot(weights[offset].T, window, preferred_element_type=jnp.float32)
        back_window = tap_window(out_grad, 2 - shift_row, 2 - shift_col)
        backward_sum = backward_sum + jnp.dot(weights[offset], back_window, preferred_element_type=jnp.float32)
    conv_out = forward_sum.reshape(GW, IMAGES, PIX).astype(jnp.bfloat16)
    in_grad = backward_sum.reshape(GW, IMAGES, PIX).astype(jnp.bfloat16)
    return (conv_out, in_grad)
```

```python
import functools

import jax
import jax.numpy as jnp
from jax import lax
from jax.experimental import pallas as pl
from jax.experimental.pallas import tpu as pltpu
from jax.sharding import PartitionSpec as P

GW = 1008
HH = 24
WW = 24
CO_SPLIT = 4
CI_SPLIT = 16
CIB = 63
TAPS = 9
SLAB = 64
LANES = 128
MESH = pl.DeviceIdType.MESH
F32 = jnp.float32
BF16 = jnp.bfloat16


def tap_window(flat, shift_row, shift_col):
    padded = jnp.pad(flat, ((0, 0), (0, 0), (WW + 1, WW + 1)))
    begin = WW + 1 + (shift_row - 1) * WW + (shift_col - 1)
    piece = padded[:, :, begin : begin + HH * WW]
    column = jnp.arange(HH * WW, dtype=jnp.int32) % WW + (shift_col - 1)
    valid = (column >= 0) & (column < WW)
    piece = jnp.where(valid[None, None, :], piece, jnp.zeros_like(piece))
    return piece.reshape(flat.shape[0], flat.shape[1] * HH * WW)


def plain_body(inputs, filters, out_grad, block_owner):
    slot_data = lax.all_gather(filters, "dp", axis=0, tiled=True)
    blocks = jnp.take(slot_data, block_owner, axis=0)
    col_block = filters.shape[3]
    w_local = blocks.reshape(CO_SPLIT, CI_SPLIT, TAPS, CIB, col_block)
    w_local = w_local.transpose(2, 1, 3, 0, 4).reshape(TAPS, GW, CO_SPLIT * col_block)
    image_total = inputs.shape[1]
    pixel_span = image_total * HH * WW
    running = jnp.zeros((w_local.shape[2], pixel_span), F32)
    portion = lax.all_gather(inputs, "filt", axis=0, tiled=True)
    for offset in range(TAPS):
        window = tap_window(portion, offset // 3, offset % 3)
        running = running + lax.dot_general(
            w_local[offset], window, (((0,), (0,)), ((), ())), preferred_element_type=F32
        )
    conv_out = running.reshape(running.shape[0], image_total, HH * WW).astype(BF16)
    total_sum = jnp.zeros((inputs.shape[0] * lax.axis_size("filt"), pixel_span), F32)
    for offset in range(TAPS):
        window = tap_window(out_grad, 2 - offset // 3, 2 - offset % 3)
        total_sum = total_sum + jnp.dot(w_local[offset], window, preferred_element_type=F32)
    result = lax.psum_scatter(total_sum, "filt", scatter_dimension=0, tiled=True)
    in_grad = result.reshape(result.shape[0], image_total, HH * WW).astype(BF16)
    return (conv_out, in_grad)


def pack_filters_kernel(f_ref, o_ref):
    half, rows, cols = o_ref.shape[1], f_ref.shape[2], f_ref.shape[3]
    o_ref[...] = jnp.zeros_like(o_ref)
    o_ref[0, :, :rows, :cols] = f_ref[:half, 0]
    o_ref[0, :, :rows, SLAB : SLAB + cols] = f_ref[half:, 0]


def pack_filters(filters):
    slots, taps, rows, cols = filters.shape
    return pl.pallas_call(
        pack_filters_kernel,
        grid=(taps,),
        in_specs=[pl.BlockSpec((slots, 1, rows, cols), lambda t: (0, t, 0, 0))],
        out_specs=pl.BlockSpec((1, slots // 2, SLAB, LANES), lambda t: (t, 0, 0, 0)),
        out_shape=jax.ShapeDtypeStruct((taps, slots // 2, SLAB, LANES), BF16),
    )(filters)


def pack_channels(x, wide):
    slabs = x.shape[0] // CIB
    x = x.reshape(slabs, CIB, x.shape[1] * x.shape[2])
    x = jnp.pad(x, ((0, 0), (0, SLAB - CIB), (0, wide - x.shape[2])))
    return x.reshape(slabs * SLAB, wide)


def main_kernel(
    D, F, w_ref, x_ref, g_ref, idx_ref, half_ref, conv_ref, grad_ref,
    wbuf, cur, xbuf, wt, accb, pair, gathered, summed,
    wsend, wrecv, xsend, xrecv, psend, precv, qsend, qrecv, lsem,
):
    me = lax.axis_index("dp")
    f = lax.axis_index("filt")
    taps, pairs = w_ref.shape[0], w_ref.shape[1]
    rows, wide = x_ref.shape
    core = lax.rem(f, 2)
    chip = f // 2
    G = F // 2

    barrier = pltpu.get_barrier_semaphore()

    @pl.when(me > 0)
    def _():
        pl.semaphore_signal(barrier, inc=1, device_id={"dp": me - 1}, device_id_type=MESH)

    @pl.when(me < D - 1)
    def _():
        pl.semaphore_signal(barrier, inc=1, device_id={"dp": me + 1}, device_id_type=MESH)

    for j in range(1, F):
        pl.semaphore_signal(barrier, inc=1, device_id={"filt": lax.rem(f + j, F)}, device_id_type=MESH)

    def slot(t, o):
        return wbuf.at[t, pl.ds(o * pairs, pairs)]

    own = pltpu.make_async_copy(w_ref, wbuf.at[:, pl.ds(me * pairs, pairs)], lsem.at[0])
    own.start()
    ownx = pltpu.make_async_copy(x_ref, xbuf.at[f], lsem.at[1])
    ownx.start()

    pl.semaphore_wait(barrier, F - 1 + jnp.minimum(me, 1) + jnp.minimum(D - 1 - me, 1))

    def send(src, t, o, side):
        to = me + 1 if side else me - 1
        return pltpu.make_async_remote_copy(
            src_ref=src, dst_ref=slot(t, o), send_sem=wsend.at[side, o, t],
            recv_sem=wrecv.at[o, t], device_id={"dp": to}, device_id_type=MESH,
        )

    def send_own(t):
        @pl.when(me < D - 1)
        def _():
            send(w_ref.at[t], t, me, 1).start()

        @pl.when(me > 0)
        def _():
            send(w_ref.at[t], t, me, 0).start()

    def xcopy(j):
        return pltpu.make_async_remote_copy(
            src_ref=x_ref, dst_ref=xbuf.at[f], send_sem=xsend.at[j],
            recv_sem=xrecv.at[F - j], device_id={"filt": lax.rem(f + j, F)}, device_id_type=MESH,
        )

    LEAD = min(2, taps)
    for t in range(LEAD):
        send_own(t)
    for j in range(1, F):
        xcopy(j).start()
    accb[...] = jnp.zeros_like(accb)
    pix = lax.broadcasted_iota(jnp.int32, (1, wide), 1)
    col = lax.rem(pix, WW)
    gathered[...] = jnp.zeros_like(gathered)
    lane = lax.broadcasted_iota(jnp.int32, (SLAB, LANES), 1)
    own.wait()
    ownx.wait()
    for j in range(1, F):
        pltpu.make_async_remote_copy(
            src_ref=x_ref, dst_ref=xbuf.at[lax.rem(f + j, F)], send_sem=xsend.at[j],
            recv_sem=xrecv.at[j], device_id={"filt": lax.rem(f + j, F)}, device_id_type=MESH,
        ).wait_recv()

    def shifted(value, dr, dc):
        off = dr * WW + dc
        moved = pltpu.roll(value.astype(F32), lax.rem(wide - off, wide), 1)
        good = (col + dc >= 0) & (col + dc < WW)
        return jnp.where(good, moved, 0.0).astype(BF16)

    def assemble(t):
        cur[...] = wbuf[t]

        def one(c, carry):
            for p in range(CO_SPLIT // 2):
                bl, br = (2 * p) * CI_SPLIT + c, (2 * p + 1) * CI_SPLIT + c
                vl = cur[idx_ref[bl]].astype(F32)
                vr = cur[idx_ref[br]].astype(F32)
                left = jnp.where(lane * 0 + half_ref[bl] == 0, vl, pltpu.roll(vl, SLAB, 1))
                right = jnp.where(lane * 0 + half_ref[br] == 1, vr, pltpu.roll(vr, SLAB, 1))
                both = jnp.where(lane < SLAB, left, right).astype(BF16)
                wt[pl.ds(pl.multiple_of(c * SLAB, SLAB), SLAB), p * LANES : (p + 1) * LANES] = both
            return carry

        lax.fori_loop(0, CI_SPLIT, one, 0)

    def backward(t):
        g = shifted(g_ref[...], 1 - t // 3, 1 - lax.rem(t, 3))
        for k in range(F):
            accb[k] += jnp.dot(wt[k * rows : (k + 1) * rows], g, preferred_element_type=F32)

    def forward(t):
        total = gathered[...]
        for k in range(F):
            x = shifted(xbuf[k], t // 3 - 1, lax.rem(t, 3) - 1)
            total += lax.dot_general(
                wt[k * rows : (k + 1) * rows], x, (((0,), (0,)), ((), ())), preferred_element_type=F32
            )
        gathered[...] = total

    def step(t, carry):
        @pl.when(t + LEAD < taps)
        def _():
            send_own(t + LEAD)

        for d in range(1, D):
            @pl.when(me - d >= 0)
            def _():
                send(slot(t, me - d), t, me - d, 1).wait_recv()

                @pl.when(me < D - 1)
                def _():
                    send(slot(t, me - d), t, me - d, 1).start()

            @pl.when(me + d < D)
            def _():
                send(slot(t, me + d), t, me + d, 0).wait_recv()

                @pl.when(me > 0)
                def _():
                    send(slot(t, me + d), t, me + d, 0).start()

        assemble(t)
        backward(t)

        @pl.when(t < taps - 1)
        def _():
            forward(t)

        return carry

    lax.fori_loop(0, taps, step, 0)

    other = chip * 2 + (1 - core)

    def pair_copy(k):
        g = lax.rem(chip + k, G)
        return pltpu.make_async_remote_copy(
            src_ref=accb.at[g * 2 + (1 - core)], dst_ref=pair.at[k], send_sem=psend.at[k],
            recv_sem=precv.at[k], device_id={"filt": other}, device_id_type=MESH,
        )

    def chip_copy(k):
        g = lax.rem(chip + k, G)
        return pltpu.make_async_remote_copy(
            src_ref=summed.at[k], dst_ref=pair.at[G + G - k], send_sem=qsend.at[k],
            recv_sem=qrecv.at[G - k], device_id={"filt": g * 2 + core}, device_id_type=MESH,
        )

    order = list(range(1, G)) + [0]
    for k in order:
        pair_copy(k).start()
    for k in order:
        g = lax.rem(chip + k, G)
        pair_copy(k).wait_recv()
        summed[k] = accb[g * 2 + core] + pair[k]
        if k:
            chip_copy(k).start()
    forward(taps - 1)
    conv_ref[...] = gathered[...].astype(BF16)
    total = summed[0]
    for k in range(1, G):
        chip_copy(k).wait_recv()
        total = total + pair[G + G - k]
    grad_ref[...] = total.astype(BF16)

    for k in range(G):
        pair_copy(k).wait_send()
    for k in range(1, G):
        chip_copy(k).wait_send()
    for j in range(1, F):
        xcopy(j).wait_send()

    def drain(t, carry):
        @pl.when(me < D - 1)
        def _():
            for d in range(D):
                @pl.when(me - d >= 0)
                def _():
                    send(slot(t, me - d), t, me - d, 1).wait_send()

        @pl.when(me > 0)
        def _():
            for d in range(D):
                @pl.when(me + d < D)
                def _():
                    send(slot(t, me + d), t, me + d, 0).wait_send()

        return carry

    lax.fori_loop(0, taps, drain, 0)


def fast_body(D, F, inputs, filters, out_grad, block_owner):
    slots, taps = filters.shape[0], filters.shape[1]
    channels, images, pixels = inputs.shape
    wide = -(-(pixels + WW + 1) // LANES) * LANES
    rows = channels // CIB * SLAB
    pairs = slots // 2
    w = pack_filters(filters)
    x = pack_channels(inputs, wide)
    g = pack_channels(out_grad, wide)
    idx = block_owner // slots * pairs + block_owner % pairs
    half = block_owner % slots // pairs
    G = F // 2
    vm = pl.BlockSpec(memory_space=pltpu.VMEM)
    sm = pl.BlockSpec(memory_space=pltpu.SMEM)
    dma = pltpu.SemaphoreType.DMA
    conv, grad = pl.pallas_call(
        functools.partial(main_kernel, D, F),
        out_shape=[jax.ShapeDtypeStruct((rows, wide), BF16)] * 2,
        in_specs=[vm, vm, vm, sm, sm],
        out_specs=[vm, vm],
        scratch_shapes=[
            pltpu.VMEM((taps, D * pairs, SLAB, LANES), BF16),
            pltpu.VMEM((D * pairs, SLAB, LANES), BF16),
            pltpu.VMEM((F, rows, wide), BF16),
            pltpu.VMEM((F * rows, rows), BF16),
            pltpu.VMEM((F, rows, wide), F32),
            pltpu.VMEM((2 * G, rows, wide), F32),
            pltpu.VMEM((rows, wide), F32),
            pltpu.VMEM((G, rows, wide), F32),
            dma((2, D, taps)), dma((D, taps)), dma((F,)), dma((F,)),
            dma((G,)), dma((G,)), dma((G + 1,)), dma((G + 1,)), dma((2,)),
        ],
        compiler_params=pltpu.CompilerParams(
            collective_id=0, has_side_effects=True, vmem_limit_bytes=60 * 1024 * 1024
        ),
    )(w, x, g, idx, half)

    def unpack(v):
        v = v.reshape(channels // CIB, SLAB, wide)[:, :CIB, :pixels]
        return v.reshape(channels, images, pixels)

    return unpack(conv), unpack(grad)


def solution(mesh):
    D, F = mesh.shape["dp"], mesh.shape["filt"]
    placed = (
        P("filt", ("parts", "dp"), None),
        P(("parts", "dp"), None, None, "filt"),
        P("filt", ("parts", "dp"), None),
        P("parts"),
    )

    def body(inputs, filters, out_grad, block_owner):
        if filters.shape[0] % 2 == 0 and F % 2 == 0 and inputs.shape[1] == 1 and D <= 8:
            return fast_body(D, F, inputs, filters, out_grad, block_owner)
        return plain_body(inputs, filters, out_grad, block_owner)

    return jax.shard_map(
        body,
        mesh=mesh,
        in_specs=placed,
        out_specs=(P("filt", ("parts", "dp"), None), P("filt", ("parts", "dp"), None)),
        check_vma=False,
    )
```

```python
import functools

import jax
import jax.numpy as jnp
from jax import lax
from jax.experimental import pallas as pl
from jax.experimental.pallas import tpu as pltpu
from jax.sharding import PartitionSpec as P

GW = 1008
HH = 24
WW = 24
CO_SPLIT = 4
CI_SPLIT = 16
CIB = 63
TAPS = 9
SLAB = 64
LANES = 128
MESH = pl.DeviceIdType.MESH
F32 = jnp.float32
BF16 = jnp.bfloat16


def tap_window(flat, shift_row, shift_col):
    padded = jnp.pad(flat, ((0, 0), (0, 0), (WW + 1, WW + 1)))
    begin = WW + 1 + (shift_row - 1) * WW + (shift_col - 1)
    piece = padded[:, :, begin : begin + HH * WW]
    column = jnp.arange(HH * WW, dtype=jnp.int32) % WW + (shift_col - 1)
    valid = (column >= 0) & (column < WW)
    piece = jnp.where(valid[None, None, :], piece, jnp.zeros_like(piece))
    return piece.reshape(flat.shape[0], flat.shape[1] * HH * WW)


def plain_body(inputs, filters, out_grad, block_owner):
    slot_data = lax.all_gather(filters, "dp", axis=0, tiled=True)
    blocks = jnp.take(slot_data, block_owner, axis=0)
    col_block = filters.shape[3]
    w_local = blocks.reshape(CO_SPLIT, CI_SPLIT, TAPS, CIB, col_block)
    w_local = w_local.transpose(2, 1, 3, 0, 4).reshape(TAPS, GW, CO_SPLIT * col_block)
    image_total = inputs.shape[1]
    pixel_span = image_total * HH * WW
    running = jnp.zeros((w_local.shape[2], pixel_span), F32)
    portion = lax.all_gather(inputs, "filt", axis=0, tiled=True)
    for offset in range(TAPS):
        window = tap_window(portion, offset // 3, offset % 3)
        running = running + lax.dot_general(
            w_local[offset], window, (((0,), (0,)), ((), ())), preferred_element_type=F32
        )
    conv_out = running.reshape(running.shape[0], image_total, HH * WW).astype(BF16)
    total_sum = jnp.zeros((inputs.shape[0] * lax.axis_size("filt"), pixel_span), F32)
    for offset in range(TAPS):
        window = tap_window(out_grad, 2 - offset // 3, 2 - offset % 3)
        total_sum = total_sum + jnp.dot(w_local[offset], window, preferred_element_type=F32)
    result = lax.psum_scatter(total_sum, "filt", scatter_dimension=0, tiled=True)
    in_grad = result.reshape(result.shape[0], image_total, HH * WW).astype(BF16)
    return (conv_out, in_grad)


def pack_filters_kernel(f_ref, o_ref):
    half, rows, cols = o_ref.shape[1], f_ref.shape[2], f_ref.shape[3]
    o_ref[...] = jnp.zeros_like(o_ref)
    for t in range(o_ref.shape[0]):
        o_ref[t, :, :rows, :cols] = f_ref[:half, t]
        o_ref[t, :, :rows, SLAB : SLAB + cols] = f_ref[half:, t]


def pack_filters(filters):
    slots, taps, rows, cols = filters.shape
    group = 3 if taps % 3 == 0 else 1
    return pl.pallas_call(
        pack_filters_kernel,
        grid=(taps // group,),
        in_specs=[pl.BlockSpec((slots, group, rows, cols), lambda t: (0, t, 0, 0))],
        out_specs=pl.BlockSpec((group, slots // 2, SLAB, LANES), lambda t: (t, 0, 0, 0)),
        out_shape=jax.ShapeDtypeStruct((taps, slots // 2, SLAB, LANES), BF16),
    )(filters)


def pack_channels_kernel(slabs, x_ref, g_ref, xo_ref, go_ref, tmp):
    pixels, channels = x_ref.shape
    lane = lax.broadcasted_iota(jnp.int32, tmp.shape, 1)
    for src, dst in ((x_ref, xo_ref), (g_ref, go_ref)):
        tmp[...] = jnp.zeros_like(tmp)
        tmp[:, :channels] = src[...].astype(F32)
        v = tmp[...]
        out = jnp.zeros_like(v)
        for k in range(slabs):
            moved = v if k == 0 else pltpu.roll(v, k, 1)
            mine = (lane >= k * SLAB) & (lane < k * SLAB + CIB)
            out = jnp.where(mine, moved, out)
        dst[...] = jnp.zeros_like(dst)
        dst[:pixels] = out.astype(BF16)


def pack_channels(x, g, tall, rows):
    vm = pl.BlockSpec(memory_space=pltpu.VMEM)
    return pl.pallas_call(
        functools.partial(pack_channels_kernel, x.shape[1] // CIB),
        in_specs=[vm, vm],
        out_specs=[vm, vm],
        out_shape=[jax.ShapeDtypeStruct((tall, rows), BF16)] * 2,
        scratch_shapes=[pltpu.VMEM((x.shape[0], rows), F32)],
    )(x, g)


def main_kernel(
    D, F, w_ref, x_ref, g_ref, idx_ref, half_ref, conv_ref, grad_ref,
    wbuf, cur, xbuf, wt, accb, pair, gathered, summed, colbuf,
    wsend, wrecv, xsend, xrecv, psend, precv, qsend, qrecv, lsem,
):
    me = lax.axis_index("dp")
    f = lax.axis_index("filt")
    taps, pairs = w_ref.shape[0], w_ref.shape[1]
    tall, rows = x_ref.shape
    pixels, channels = conv_ref.shape
    core = lax.rem(f, 2)
    chip = f // 2
    G = F // 2

    barrier = pltpu.get_barrier_semaphore()

    @pl.when(me > 0)
    def _():
        pl.semaphore_signal(barrier, inc=1, device_id={"dp": me - 1}, device_id_type=MESH)

    @pl.when(me < D - 1)
    def _():
        pl.semaphore_signal(barrier, inc=1, device_id={"dp": me + 1}, device_id_type=MESH)

    for j in range(1, F):
        pl.semaphore_signal(barrier, inc=1, device_id={"filt": lax.rem(f + j, F)}, device_id_type=MESH)

    def slot(t, o):
        return wbuf.at[t, pl.ds(o * pairs, pairs)]

    own = pltpu.make_async_copy(w_ref, wbuf.at[:, pl.ds(me * pairs, pairs)], lsem.at[0])
    own.start()
    ownx = pltpu.make_async_copy(x_ref, xbuf.at[f], lsem.at[1])
    ownx.start()

    pl.semaphore_wait(barrier, F - 1 + jnp.minimum(me, 1) + jnp.minimum(D - 1 - me, 1))

    def send(src, t, o, side):
        to = me + 1 if side else me - 1
        return pltpu.make_async_remote_copy(
            src_ref=src, dst_ref=slot(t, o), send_sem=wsend.at[side, o, t],
            recv_sem=wrecv.at[o, t], device_id={"dp": to}, device_id_type=MESH,
        )

    def send_own(t):
        @pl.when(me < D - 1)
        def _():
            send(w_ref.at[t], t, me, 1).start()

        @pl.when(me > 0)
        def _():
            send(w_ref.at[t], t, me, 0).start()

    def xcopy(j):
        return pltpu.make_async_remote_copy(
            src_ref=x_ref, dst_ref=xbuf.at[f], send_sem=xsend.at[j],
            recv_sem=xrecv.at[F - j], device_id={"filt": lax.rem(f + j, F)}, device_id_type=MESH,
        )

    LEAD = min(4, taps)
    for t in range(LEAD):
        send_own(t)
    for j in range(1, F):
        xcopy(j).start()
    accb[...] = jnp.zeros_like(accb)
    colbuf[...] = lax.rem(lax.broadcasted_iota(jnp.int32, (tall, rows), 0), WW)
    gathered[...] = jnp.zeros_like(gathered)
    lane = lax.broadcasted_iota(jnp.int32, (SLAB, LANES), 1)
    own.wait()
    ownx.wait()
    def shifted(value, dr, dc):
        off = dr * WW + dc
        moved = pltpu.roll(value.astype(F32), lax.rem(tall - off, tall), 0)
        col = colbuf[...] + dc
        good = (col >= 0) & (col < WW)
        return jnp.where(good, moved, 0.0).astype(BF16)

    def assemble(t):
        cur[...] = wbuf[t]

        def one(c, carry):
            for p in range(CO_SPLIT // 2):
                bl, br = (2 * p) * CI_SPLIT + c, (2 * p + 1) * CI_SPLIT + c
                vl = cur[idx_ref[bl]].astype(F32)
                vr = cur[idx_ref[br]].astype(F32)
                left = jnp.where(lane * 0 + half_ref[bl] == 0, vl, pltpu.roll(vl, SLAB, 1))
                right = jnp.where(lane * 0 + half_ref[br] == 1, vr, pltpu.roll(vr, SLAB, 1))
                both = jnp.where(lane < SLAB, left, right).astype(BF16)
                wt[pl.ds(pl.multiple_of(c * SLAB, SLAB), SLAB), p * LANES : (p + 1) * LANES] = both
            return carry

        lax.fori_loop(0, CI_SPLIT, one, 0)

    def backward(t):
        g = shifted(g_ref[...], 1 - t // 3, 1 - lax.rem(t, 3))
        for k in range(F):
            accb[k] += lax.dot_general(
                g, wt[k * rows : (k + 1) * rows], (((1,), (1,)), ((), ())), preferred_element_type=F32
            )

    def forward(t):
        total = gathered[...]
        for k in range(F):
            x = shifted(xbuf[k], t // 3 - 1, lax.rem(t, 3) - 1)
            total += jnp.dot(x, wt[k * rows : (k + 1) * rows], preferred_element_type=F32)
        gathered[...] = total

    def step(t, carry):
        @pl.when(t + LEAD < taps)
        def _():
            send_own(t + LEAD)

        for d in range(1, D):
            @pl.when(me - d >= 0)
            def _():
                send(slot(t, me - d), t, me - d, 1).wait_recv()

                @pl.when(me < D - 1)
                def _():
                    send(slot(t, me - d), t, me - d, 1).start()

            @pl.when(me + d < D)
            def _():
                send(slot(t, me + d), t, me + d, 0).wait_recv()

                @pl.when(me > 0)
                def _():
                    send(slot(t, me + d), t, me + d, 0).start()

        assemble(t)
        backward(t)

        @pl.when(t == 0)
        def _():
            for j in range(1, F):
                pltpu.make_async_remote_copy(
                    src_ref=x_ref, dst_ref=xbuf.at[lax.rem(f + j, F)], send_sem=xsend.at[j],
                    recv_sem=xrecv.at[j], device_id={"filt": lax.rem(f + j, F)}, device_id_type=MESH,
                ).wait_recv()

        @pl.when(t < taps - 1)
        def _():
            forward(t)

        return carry

    lax.fori_loop(0, taps, step, 0)

    other = chip * 2 + (1 - core)

    def pair_copy(k):
        g = lax.rem(chip + k, G)
        return pltpu.make_async_remote_copy(
            src_ref=accb.at[g * 2 + (1 - core), pl.ds(0, pixels)], dst_ref=pair.at[k], send_sem=psend.at[k],
            recv_sem=precv.at[k], device_id={"filt": other}, device_id_type=MESH,
        )

    def chip_copy(k):
        g = lax.rem(chip + k, G)
        return pltpu.make_async_remote_copy(
            src_ref=summed.at[k], dst_ref=pair.at[G + G - k], send_sem=qsend.at[k],
            recv_sem=qrecv.at[G - k], device_id={"filt": g * 2 + core}, device_id_type=MESH,
        )

    order = list(range(1, G)) + [0]
    for k in order:
        pair_copy(k).start()
    for k in order:
        g = lax.rem(chip + k, G)
        pair_copy(k).wait_recv()
        summed[k] = accb[g * 2 + core, :pixels] + pair[k]
        if k:
            chip_copy(k).start()
    forward(taps - 1)
    lanes = lax.broadcasted_iota(jnp.int32, (pixels, rows), 1)

    def closed(v):
        out = v
        for k in range(1, channels // CIB):
            out = jnp.where(lanes >= k * CIB, pltpu.roll(v, rows - k, 1), out)
        return out.astype(BF16)[:, :channels]

    conv_ref[...] = closed(gathered[:pixels])
    total = summed[0]
    for k in range(1, G):
        chip_copy(k).wait_recv()
        total = total + pair[G + G - k]
    grad_ref[...] = closed(total)

    for k in range(G):
        pair_copy(k).wait_send()
    for k in range(1, G):
        chip_copy(k).wait_send()
    for j in range(1, F):
        xcopy(j).wait_send()

    def drain(t, carry):
        @pl.when(me < D - 1)
        def _():
            for d in range(D):
                @pl.when(me - d >= 0)
                def _():
                    send(slot(t, me - d), t, me - d, 1).wait_send()

        @pl.when(me > 0)
        def _():
            for d in range(D):
                @pl.when(me + d < D)
                def _():
                    send(slot(t, me + d), t, me + d, 0).wait_send()

        return carry

    lax.fori_loop(0, taps, drain, 0)


def fast_body(D, F, inputs, filters, out_grad, block_owner):
    slots, taps = filters.shape[0], filters.shape[1]
    channels, images, pixels = inputs.shape
    tall = -(-(pixels + WW + 1) // 32) * 32
    rows = channels // CIB * SLAB
    pairs = slots // 2
    w = pack_filters(filters)
    x, g = pack_channels(inputs[:, 0].T, out_grad[:, 0].T, tall, rows)
    idx = block_owner // slots * pairs + block_owner % pairs
    half = block_owner % slots // pairs
    G = F // 2
    vm = pl.BlockSpec(memory_space=pltpu.VMEM)
    sm = pl.BlockSpec(memory_space=pltpu.SMEM)
    dma = pltpu.SemaphoreType.DMA
    conv, grad = pl.pallas_call(
        functools.partial(main_kernel, D, F),
        out_shape=[jax.ShapeDtypeStruct((pixels, channels), BF16)] * 2,
        in_specs=[vm, vm, vm, sm, sm],
        out_specs=[vm, vm],
        scratch_shapes=[
            pltpu.VMEM((taps, D * pairs, SLAB, LANES), BF16),
            pltpu.VMEM((D * pairs, SLAB, LANES), BF16),
            pltpu.VMEM((F, tall, rows), BF16),
            pltpu.VMEM((F * rows, rows), BF16),
            pltpu.VMEM((F, tall, rows), F32),
            pltpu.VMEM((2 * G, pixels, rows), F32),
            pltpu.VMEM((tall, rows), F32),
            pltpu.VMEM((G, pixels, rows), F32),
            pltpu.VMEM((tall, rows), jnp.int32),
            dma((2, D, taps)), dma((D, taps)), dma((F,)), dma((F,)),
            dma((G,)), dma((G,)), dma((G + 1,)), dma((G + 1,)), dma((2,)),
        ],
        compiler_params=pltpu.CompilerParams(
            collective_id=0, has_side_effects=True, vmem_limit_bytes=60 * 1024 * 1024
        ),
    )(w, x, g, idx, half)

    return conv.T[:, None], grad.T[:, None]


def solution(mesh):
    D, F = mesh.shape["dp"], mesh.shape["filt"]
    placed = (
        P("filt", ("parts", "dp"), None),
        P(("parts", "dp"), None, None, "filt"),
        P("filt", ("parts", "dp"), None),
        P("parts"),
    )

    def body(inputs, filters, out_grad, block_owner):
        if filters.shape[0] % 2 == 0 and F % 2 == 0 and inputs.shape[1] == 1 and D <= 8:
            return fast_body(D, F, inputs, filters, out_grad, block_owner)
        return plain_body(inputs, filters, out_grad, block_owner)

    return jax.shard_map(
        body,
        mesh=mesh,
        in_specs=placed,
        out_specs=(P("filt", ("parts", "dp"), None), P("filt", ("parts", "dp"), None)),
        check_vma=False,
    )
```

```python
import functools

import jax
import jax.numpy as jnp
from jax import lax
from jax.experimental import pallas as pl
from jax.experimental.pallas import tpu as pltpu
from jax.sharding import PartitionSpec as P

GW = 1008
HH = 24
WW = 24
CO_SPLIT = 4
CI_SPLIT = 16
CIB = 63
TAPS = 9
SLAB = 64
LANES = 128
MESH = pl.DeviceIdType.MESH
F32 = jnp.float32
BF16 = jnp.bfloat16


def tap_window(flat, shift_row, shift_col):
    padded = jnp.pad(flat, ((0, 0), (0, 0), (WW + 1, WW + 1)))
    begin = WW + 1 + (shift_row - 1) * WW + (shift_col - 1)
    piece = padded[:, :, begin : begin + HH * WW]
    column = jnp.arange(HH * WW, dtype=jnp.int32) % WW + (shift_col - 1)
    valid = (column >= 0) & (column < WW)
    piece = jnp.where(valid[None, None, :], piece, jnp.zeros_like(piece))
    return piece.reshape(flat.shape[0], flat.shape[1] * HH * WW)


def plain_body(inputs, filters, out_grad, block_owner):
    slot_data = lax.all_gather(filters, "dp", axis=0, tiled=True)
    blocks = jnp.take(slot_data, block_owner, axis=0)
    col_block = filters.shape[3]
    w_local = blocks.reshape(CO_SPLIT, CI_SPLIT, TAPS, CIB, col_block)
    w_local = w_local.transpose(2, 1, 3, 0, 4).reshape(TAPS, GW, CO_SPLIT * col_block)
    image_total = inputs.shape[1]
    pixel_span = image_total * HH * WW
    running = jnp.zeros((w_local.shape[2], pixel_span), F32)
    portion = lax.all_gather(inputs, "filt", axis=0, tiled=True)
    for offset in range(TAPS):
        window = tap_window(portion, offset // 3, offset % 3)
        running = running + lax.dot_general(
            w_local[offset], window, (((0,), (0,)), ((), ())), preferred_element_type=F32
        )
    conv_out = running.reshape(running.shape[0], image_total, HH * WW).astype(BF16)
    total_sum = jnp.zeros((inputs.shape[0] * lax.axis_size("filt"), pixel_span), F32)
    for offset in range(TAPS):
        window = tap_window(out_grad, 2 - offset // 3, 2 - offset % 3)
        total_sum = total_sum + jnp.dot(w_local[offset], window, preferred_element_type=F32)
    result = lax.psum_scatter(total_sum, "filt", scatter_dimension=0, tiled=True)
    in_grad = result.reshape(result.shape[0], image_total, HH * WW).astype(BF16)
    return (conv_out, in_grad)


def pack_filters_kernel(f_ref, o_ref):
    half, rows, cols = o_ref.shape[1], f_ref.shape[2], f_ref.shape[3]
    o_ref[...] = jnp.zeros_like(o_ref)
    for t in range(o_ref.shape[0]):
        o_ref[t, :, :rows, :cols] = f_ref[:half, t]
        o_ref[t, :, :rows, SLAB : SLAB + cols] = f_ref[half:, t]


def pack_filters(filters):
    slots, taps, rows, cols = filters.shape
    group = 3 if taps % 3 == 0 else 1
    return pl.pallas_call(
        pack_filters_kernel,
        grid=(taps // group,),
        in_specs=[pl.BlockSpec((slots, group, rows, cols), lambda t: (0, t, 0, 0))],
        out_specs=pl.BlockSpec((group, slots // 2, SLAB, LANES), lambda t: (t, 0, 0, 0)),
        out_shape=jax.ShapeDtypeStruct((taps, slots // 2, SLAB, LANES), BF16),
    )(filters)


def pack_channels_kernel(slabs, x_ref, g_ref, xo_ref, go_ref, tmp):
    channels = x_ref.shape[1]
    lane = lax.broadcasted_iota(jnp.int32, tmp.shape, 1)
    for src, dst in ((x_ref, xo_ref), (g_ref, go_ref)):
        tmp[...] = jnp.zeros_like(tmp)
        tmp[:, :channels] = src[...].astype(F32)
        v = tmp[...]
        out = jnp.zeros_like(v)
        for k in range(slabs):
            moved = v if k == 0 else pltpu.roll(v, k, 1)
            mine = (lane >= k * SLAB) & (lane < k * SLAB + CIB)
            out = jnp.where(mine, moved, out)
        dst[...] = out.astype(BF16)


def pack_channels(x, g, tall, rows):
    vm = pl.BlockSpec(memory_space=pltpu.VMEM)
    return pl.pallas_call(
        functools.partial(pack_channels_kernel, x.shape[1] // CIB),
        in_specs=[vm, vm],
        out_specs=[vm, vm],
        out_shape=[jax.ShapeDtypeStruct((tall, rows), BF16)] * 2,
        scratch_shapes=[pltpu.VMEM((x.shape[0], rows), F32)],
    )(x, g)


def main_kernel(
    D, F, w_ref, x_ref, g_ref, idx_ref, half_ref, conv_ref, grad_ref,
    wbuf, cur, xbuf, wt, accb, pair, gathered, summed, gsh, xsh,
    wsend, wrecv, xsend, xrecv, psend, precv, qsend, qrecv, lsem,
):
    me = lax.axis_index("dp")
    f = lax.axis_index("filt")
    taps, pairs = w_ref.shape[0], w_ref.shape[1]
    tall, rows = x_ref.shape
    pixels, channels = conv_ref.shape
    core = lax.rem(f, 2)
    chip = f // 2
    G = F // 2

    barrier = pltpu.get_barrier_semaphore()

    @pl.when(me > 0)
    def _():
        pl.semaphore_signal(barrier, inc=1, device_id={"dp": me - 1}, device_id_type=MESH)

    @pl.when(me < D - 1)
    def _():
        pl.semaphore_signal(barrier, inc=1, device_id={"dp": me + 1}, device_id_type=MESH)

    for j in range(1, F):
        pl.semaphore_signal(barrier, inc=1, device_id={"filt": lax.rem(f + j, F)}, device_id_type=MESH)

    def slot(t, o):
        return wbuf.at[t, pl.ds(o * pairs, pairs)]

    own = pltpu.make_async_copy(w_ref, wbuf.at[:, pl.ds(me * pairs, pairs)], lsem.at[0])
    own.start()
    ownx = pltpu.make_async_copy(x_ref, xbuf.at[f], lsem.at[1])
    ownx.start()

    pl.semaphore_wait(barrier, F - 1 + jnp.minimum(me, 1) + jnp.minimum(D - 1 - me, 1))

    def send(src, t, o, side):
        to = me + 1 if side else me - 1
        return pltpu.make_async_remote_copy(
            src_ref=src, dst_ref=slot(t, o), send_sem=wsend.at[side, o, t],
            recv_sem=wrecv.at[o, t], device_id={"dp": to}, device_id_type=MESH,
        )

    def send_own(t):
        @pl.when(me < D - 1)
        def _():
            send(w_ref.at[t], t, me, 1).start()

        @pl.when(me > 0)
        def _():
            send(w_ref.at[t], t, me, 0).start()

    def xcopy(j):
        return pltpu.make_async_remote_copy(
            src_ref=x_ref, dst_ref=xbuf.at[f], send_sem=xsend.at[j],
            recv_sem=xrecv.at[F - j], device_id={"filt": lax.rem(f + j, F)}, device_id_type=MESH,
        )

    LEAD = min(4, taps)
    for t in range(LEAD):
        send_own(t)
    for j in range(1, F):
        xcopy(j).start()
    accb[...] = jnp.zeros_like(accb)
    gathered[...] = jnp.zeros_like(gathered)
    lane = lax.broadcasted_iota(jnp.int32, (SLAB, LANES), 1)
    own.wait()
    ownx.wait()
    col = lax.rem(lax.broadcasted_iota(jnp.int32, (tall, rows), 0), WW)

    def spread(value, dst, lo):
        v = value.astype(F32)
        for j in range(3):
            dc = j - 1
            moved = v if dc == 0 else pltpu.roll(v, (tall - dc) % tall, 0)
            good = (col + dc >= 0) & (col + dc < WW)
            dst[j, WW : WW + tall, lo : lo + rows] = jnp.where(good, moved, 0.0)

    for buf in (gsh, xsh):
        edge = jnp.zeros((3, WW, buf.shape[2]), F32)
        buf[:, :WW] = edge
        buf[:, WW + tall :] = edge
    spread(g_ref[...], gsh, 0)

    def window(buf, r, c):
        return buf[c, pl.ds(pl.multiple_of(r * WW, WW), tall)].astype(BF16)

    def assemble(t):
        cur[...] = wbuf[t]

        def one(c, carry):
            for p in range(CO_SPLIT // 2):
                bl, br = (2 * p) * CI_SPLIT + c, (2 * p + 1) * CI_SPLIT + c
                vl = cur[idx_ref[bl]].astype(F32)
                vr = cur[idx_ref[br]].astype(F32)
                left = jnp.where(lane * 0 + half_ref[bl] == 0, vl, pltpu.roll(vl, SLAB, 1))
                right = jnp.where(lane * 0 + half_ref[br] == 1, vr, pltpu.roll(vr, SLAB, 1))
                both = jnp.where(lane < SLAB, left, right).astype(BF16)
                wt[pl.ds(pl.multiple_of(c * SLAB, SLAB), SLAB), p * LANES : (p + 1) * LANES] = both
            return carry

        lax.fori_loop(0, CI_SPLIT, one, 0, unroll=4)

    def backward(t):
        g = window(gsh, 2 - t // 3, 2 - lax.rem(t, 3))
        for k in range(F):
            accb[k] += lax.dot_general(
                g, wt[k * rows : (k + 1) * rows], (((1,), (1,)), ((), ())), preferred_element_type=F32
            )

    def forward(t):
        x = window(xsh, t // 3, lax.rem(t, 3))
        gathered[...] += jnp.dot(x, wt[...], preferred_element_type=F32)

    def step(t, carry):
        @pl.when(t + LEAD < taps)
        def _():
            send_own(t + LEAD)

        for d in range(1, D):
            @pl.when(me - d >= 0)
            def _():
                send(slot(t, me - d), t, me - d, 1).wait_recv()

                @pl.when(me < D - 1)
                def _():
                    send(slot(t, me - d), t, me - d, 1).start()

            @pl.when(me + d < D)
            def _():
                send(slot(t, me + d), t, me + d, 0).wait_recv()

                @pl.when(me > 0)
                def _():
                    send(slot(t, me + d), t, me + d, 0).start()

        assemble(t)
        backward(t)

        @pl.when(t == 0)
        def _():
            for j in range(1, F):
                pltpu.make_async_remote_copy(
                    src_ref=x_ref, dst_ref=xbuf.at[lax.rem(f + j, F)], send_sem=xsend.at[j],
                    recv_sem=xrecv.at[j], device_id={"filt": lax.rem(f + j, F)}, device_id_type=MESH,
                ).wait_recv()
            for k in range(F):
                spread(xbuf[k], xsh, k * rows)

        @pl.when(t < taps - 1)
        def _():
            forward(t)

        return carry

    lax.fori_loop(0, taps, step, 0)

    other = chip * 2 + (1 - core)

    def pair_copy(k):
        g = lax.rem(chip + k, G)
        return pltpu.make_async_remote_copy(
            src_ref=accb.at[g * 2 + (1 - core), pl.ds(0, pixels)], dst_ref=pair.at[k], send_sem=psend.at[k],
            recv_sem=precv.at[k], device_id={"filt": other}, device_id_type=MESH,
        )

    def chip_copy(k):
        g = lax.rem(chip + k, G)
        return pltpu.make_async_remote_copy(
            src_ref=summed.at[k], dst_ref=pair.at[G + G - k], send_sem=qsend.at[k],
            recv_sem=qrecv.at[G - k], device_id={"filt": g * 2 + core}, device_id_type=MESH,
        )

    order = list(range(1, G)) + [0]
    for k in order:
        pair_copy(k).start()
    for k in order:
        g = lax.rem(chip + k, G)
        pair_copy(k).wait_recv()
        summed[k] = accb[g * 2 + core, :pixels] + pair[k]
        if k:
            chip_copy(k).start()
    forward(taps - 1)
    lanes = lax.broadcasted_iota(jnp.int32, (pixels, rows), 1)

    def closed(v):
        out = v
        for k in range(1, channels // CIB):
            out = jnp.where(lanes >= k * CIB, pltpu.roll(v, rows - k, 1), out)
        return out.astype(BF16)[:, :channels]

    conv_ref[...] = closed(gathered[:pixels])
    total = summed[0]
    for k in range(1, G):
        chip_copy(k).wait_recv()
        total = total + pair[G + G - k]
    grad_ref[...] = closed(total)

    for k in range(G):
        pair_copy(k).wait_send()
    for k in range(1, G):
        chip_copy(k).wait_send()
    for j in range(1, F):
        xcopy(j).wait_send()

    def drain(t, carry):
        @pl.when(me < D - 1)
        def _():
            for d in range(D):
                @pl.when(me - d >= 0)
                def _():
                    send(slot(t, me - d), t, me - d, 1).wait_send()

        @pl.when(me > 0)
        def _():
            for d in range(D):
                @pl.when(me + d < D)
                def _():
                    send(slot(t, me + d), t, me + d, 0).wait_send()

        return carry

    lax.fori_loop(0, taps, drain, 0)


def fast_body(D, F, inputs, filters, out_grad, block_owner):
    slots, taps = filters.shape[0], filters.shape[1]
    channels, images, pixels = inputs.shape
    tall = pixels
    rows = channels // CIB * SLAB
    pairs = slots // 2
    w = pack_filters(filters)
    x, g = pack_channels(inputs[:, 0].T, out_grad[:, 0].T, tall, rows)
    idx = block_owner // slots * pairs + block_owner % pairs
    half = block_owner % slots // pairs
    G = F // 2
    vm = pl.BlockSpec(memory_space=pltpu.VMEM)
    sm = pl.BlockSpec(memory_space=pltpu.SMEM)
    dma = pltpu.SemaphoreType.DMA
    conv, grad = pl.pallas_call(
        functools.partial(main_kernel, D, F),
        out_shape=[jax.ShapeDtypeStruct((pixels, channels), BF16)] * 2,
        in_specs=[vm, vm, vm, sm, sm],
        out_specs=[vm, vm],
        scratch_shapes=[
            pltpu.VMEM((taps, D * pairs, SLAB, LANES), BF16),
            pltpu.VMEM((D * pairs, SLAB, LANES), BF16),
            pltpu.VMEM((F, tall, rows), BF16),
            pltpu.VMEM((F * rows, rows), BF16),
            pltpu.VMEM((F, tall, rows), F32),
            pltpu.VMEM((2 * G, pixels, rows), F32),
            pltpu.VMEM((tall, rows), F32),
            pltpu.VMEM((G, pixels, rows), F32),
            pltpu.VMEM((3, tall + 2 * WW, rows), F32),
            pltpu.VMEM((3, tall + 2 * WW, F * rows), F32),
            dma((2, D, taps)), dma((D, taps)), dma((F,)), dma((F,)),
            dma((G,)), dma((G,)), dma((G + 1,)), dma((G + 1,)), dma((2,)),
        ],
        compiler_params=pltpu.CompilerParams(
            collective_id=0, has_side_effects=True, vmem_limit_bytes=60 * 1024 * 1024
        ),
    )(w, x, g, idx, half)

    return conv.T[:, None], grad.T[:, None]


def solution(mesh):
    D, F = mesh.shape["dp"], mesh.shape["filt"]
    placed = (
        P("filt", ("parts", "dp"), None),
        P(("parts", "dp"), None, None, "filt"),
        P("filt", ("parts", "dp"), None),
        P("parts"),
    )

    def body(inputs, filters, out_grad, block_owner):
        if filters.shape[0] % 2 == 0 and F % 2 == 0 and inputs.shape[1] == 1 and D <= 8:
            return fast_body(D, F, inputs, filters, out_grad, block_owner)
        return plain_body(inputs, filters, out_grad, block_owner)

    return jax.shard_map(
        body,
        mesh=mesh,
        in_specs=placed,
        out_specs=(P("filt", ("parts", "dp"), None), P("filt", ("parts", "dp"), None)),
        check_vma=False,
    )
```

```python
import functools

import jax
import jax.numpy as jnp
from jax import lax
from jax.experimental import pallas as pl
from jax.experimental.pallas import tpu as pltpu
from jax.sharding import PartitionSpec as P

GW = 1008
HH = 24
WW = 24
CO_SPLIT = 4
CI_SPLIT = 16
CIB = 63
TAPS = 9
SLAB = 64
LANES = 128
MESH = pl.DeviceIdType.MESH
F32 = jnp.float32
BF16 = jnp.bfloat16


def tap_window(flat, shift_row, shift_col):
    padded = jnp.pad(flat, ((0, 0), (0, 0), (WW + 1, WW + 1)))
    begin = WW + 1 + (shift_row - 1) * WW + (shift_col - 1)
    piece = padded[:, :, begin : begin + HH * WW]
    column = jnp.arange(HH * WW, dtype=jnp.int32) % WW + (shift_col - 1)
    valid = (column >= 0) & (column < WW)
    piece = jnp.where(valid[None, None, :], piece, jnp.zeros_like(piece))
    return piece.reshape(flat.shape[0], flat.shape[1] * HH * WW)


def plain_body(inputs, filters, out_grad, block_owner):
    slot_data = lax.all_gather(filters, "dp", axis=0, tiled=True)
    blocks = jnp.take(slot_data, block_owner, axis=0)
    col_block = filters.shape[3]
    w_local = blocks.reshape(CO_SPLIT, CI_SPLIT, TAPS, CIB, col_block)
    w_local = w_local.transpose(2, 1, 3, 0, 4).reshape(TAPS, GW, CO_SPLIT * col_block)
    image_total = inputs.shape[1]
    pixel_span = image_total * HH * WW
    running = jnp.zeros((w_local.shape[2], pixel_span), F32)
    portion = lax.all_gather(inputs, "filt", axis=0, tiled=True)
    for offset in range(TAPS):
        window = tap_window(portion, offset // 3, offset % 3)
        running = running + lax.dot_general(
            w_local[offset], window, (((0,), (0,)), ((), ())), preferred_element_type=F32
        )
    conv_out = running.reshape(running.shape[0], image_total, HH * WW).astype(BF16)
    total_sum = jnp.zeros((inputs.shape[0] * lax.axis_size("filt"), pixel_span), F32)
    for offset in range(TAPS):
        window = tap_window(out_grad, 2 - offset // 3, 2 - offset % 3)
        total_sum = total_sum + jnp.dot(w_local[offset], window, preferred_element_type=F32)
    result = lax.psum_scatter(total_sum, "filt", scatter_dimension=0, tiled=True)
    in_grad = result.reshape(result.shape[0], image_total, HH * WW).astype(BF16)
    return (conv_out, in_grad)


def pack_filters_kernel(f_ref, o_ref):
    half, rows, cols = o_ref.shape[1], f_ref.shape[2], f_ref.shape[3]
    o_ref[...] = jnp.zeros_like(o_ref)
    for t in range(o_ref.shape[0]):
        o_ref[t, :, :rows, :cols] = f_ref[:half, t]
        o_ref[t, :, :rows, SLAB : SLAB + cols] = f_ref[half:, t]


def pack_filters(filters):
    slots, taps, rows, cols = filters.shape
    group = 3 if taps % 3 == 0 else 1
    return pl.pallas_call(
        pack_filters_kernel,
        grid=(taps // group,),
        in_specs=[pl.BlockSpec((slots, group, rows, cols), lambda t: (0, t, 0, 0))],
        out_specs=pl.BlockSpec((group, slots // 2, SLAB, LANES), lambda t: (t, 0, 0, 0)),
        out_shape=jax.ShapeDtypeStruct((taps, slots // 2, SLAB, LANES), BF16),
    )(filters)


def main_kernel(
    D, F, w_ref, x_ref, g_ref, idx_ref, half_ref, conv_ref, grad_ref,
    wbuf, cur, xbuf, wt, accb, pair, gathered, summed, gsh, xsh, tmp,
    wsend, wrecv, xsend, xrecv, psend, precv, qsend, qrecv, lsem,
):
    me = lax.axis_index("dp")
    f = lax.axis_index("filt")
    taps, pairs = w_ref.shape[0], w_ref.shape[1]
    tall, channels = x_ref.shape
    pixels, rows = tall, wt.shape[1]
    core = lax.rem(f, 2)
    chip = f // 2
    G = F // 2

    barrier = pltpu.get_barrier_semaphore()

    @pl.when(me > 0)
    def _():
        pl.semaphore_signal(barrier, inc=1, device_id={"dp": me - 1}, device_id_type=MESH)

    @pl.when(me < D - 1)
    def _():
        pl.semaphore_signal(barrier, inc=1, device_id={"dp": me + 1}, device_id_type=MESH)

    for j in range(1, F):
        pl.semaphore_signal(barrier, inc=1, device_id={"filt": lax.rem(f + j, F)}, device_id_type=MESH)

    def slot(t, o):
        return wbuf.at[t, pl.ds(o * pairs, pairs)]

    own = pltpu.make_async_copy(w_ref, wbuf.at[:, pl.ds(me * pairs, pairs)], lsem.at[0])
    own.start()
    ownx = pltpu.make_async_copy(x_ref, xbuf.at[f], lsem.at[1])
    ownx.start()

    pl.semaphore_wait(barrier, F - 1 + jnp.minimum(me, 1) + jnp.minimum(D - 1 - me, 1))

    def send(src, t, o, side):
        to = me + 1 if side else me - 1
        return pltpu.make_async_remote_copy(
            src_ref=src, dst_ref=slot(t, o), send_sem=wsend.at[side, o, t],
            recv_sem=wrecv.at[o, t], device_id={"dp": to}, device_id_type=MESH,
        )

    def send_own(t):
        @pl.when(me < D - 1)
        def _():
            send(w_ref.at[t], t, me, 1).start()

        @pl.when(me > 0)
        def _():
            send(w_ref.at[t], t, me, 0).start()

    def xcopy(j):
        return pltpu.make_async_remote_copy(
            src_ref=x_ref, dst_ref=xbuf.at[f], send_sem=xsend.at[j],
            recv_sem=xrecv.at[F - j], device_id={"filt": lax.rem(f + j, F)}, device_id_type=MESH,
        )

    LEAD = min(4, taps)
    for t in range(LEAD):
        send_own(t)
    for j in range(1, F):
        xcopy(j).start()
    accb[...] = jnp.zeros_like(accb)
    gathered[...] = jnp.zeros_like(gathered)
    lane = lax.broadcasted_iota(jnp.int32, (SLAB, LANES), 1)
    own.wait()
    ownx.wait()
    col = lax.rem(lax.broadcasted_iota(jnp.int32, (tall, rows), 0), WW)

    chan = lax.broadcasted_iota(jnp.int32, (tall, rows), 1)
    tmp[...] = jnp.zeros_like(tmp)

    def spread(value, dst, lo):
        tmp[:, :channels] = value.astype(F32)
        raw = tmp[...]
        v = jnp.zeros_like(raw)
        for k in range(channels // CIB):
            moved = raw if k == 0 else pltpu.roll(raw, k, 1)
            mine = (chan >= k * SLAB) & (chan < k * SLAB + CIB)
            v = jnp.where(mine, moved, v)
        for j in range(3):
            dc = j - 1
            moved = v if dc == 0 else pltpu.roll(v, (tall - dc) % tall, 0)
            good = (col + dc >= 0) & (col + dc < WW)
            dst[j, WW : WW + tall, lo : lo + rows] = jnp.where(good, moved, 0.0)

    for buf in (gsh, xsh):
        edge = jnp.zeros((3, WW, buf.shape[2]), F32)
        buf[:, :WW] = edge
        buf[:, WW + tall :] = edge
    spread(g_ref[...], gsh, 0)

    def window(buf, r, c):
        return buf[c, pl.ds(pl.multiple_of(r * WW, WW), tall)].astype(BF16)

    def assemble(t):
        cur[...] = wbuf[t]

        def one(c, carry):
            for p in range(CO_SPLIT // 2):
                bl, br = (2 * p) * CI_SPLIT + c, (2 * p + 1) * CI_SPLIT + c
                vl = cur[idx_ref[bl]].astype(F32)
                vr = cur[idx_ref[br]].astype(F32)
                left = jnp.where(lane * 0 + half_ref[bl] == 0, vl, pltpu.roll(vl, SLAB, 1))
                right = jnp.where(lane * 0 + half_ref[br] == 1, vr, pltpu.roll(vr, SLAB, 1))
                both = jnp.where(lane < SLAB, left, right).astype(BF16)
                wt[pl.ds(pl.multiple_of(c * SLAB, SLAB), SLAB), p * LANES : (p + 1) * LANES] = both
            return carry

        lax.fori_loop(0, CI_SPLIT, one, 0, unroll=4)

    def backward(t):
        g = window(gsh, 2 - t // 3, 2 - lax.rem(t, 3))
        for k in range(F):
            accb[k] += lax.dot_general(
                g, wt[k * rows : (k + 1) * rows], (((1,), (1,)), ((), ())), preferred_element_type=F32
            )

    def forward(t):
        x = window(xsh, t // 3, lax.rem(t, 3))
        gathered[...] += jnp.dot(x, wt[...], preferred_element_type=F32)

    def step(t, carry):
        @pl.when(t + LEAD < taps)
        def _():
            send_own(t + LEAD)

        for d in range(1, D):
            @pl.when(me - d >= 0)
            def _():
                send(slot(t, me - d), t, me - d, 1).wait_recv()

                @pl.when(me < D - 1)
                def _():
                    send(slot(t, me - d), t, me - d, 1).start()

            @pl.when(me + d < D)
            def _():
                send(slot(t, me + d), t, me + d, 0).wait_recv()

                @pl.when(me > 0)
                def _():
                    send(slot(t, me + d), t, me + d, 0).start()

        assemble(t)
        backward(t)

        @pl.when(t == 0)
        def _():
            for j in range(1, F):
                pltpu.make_async_remote_copy(
                    src_ref=x_ref, dst_ref=xbuf.at[lax.rem(f + j, F)], send_sem=xsend.at[j],
                    recv_sem=xrecv.at[j], device_id={"filt": lax.rem(f + j, F)}, device_id_type=MESH,
                ).wait_recv()
            for k in range(F):
                spread(xbuf[k], xsh, k * rows)

        @pl.when(t < taps - 1)
        def _():
            forward(t)

        return carry

    lax.fori_loop(0, taps, step, 0)

    other = chip * 2 + (1 - core)

    def pair_copy(k):
        g = lax.rem(chip + k, G)
        return pltpu.make_async_remote_copy(
            src_ref=accb.at[g * 2 + (1 - core), pl.ds(0, pixels)], dst_ref=pair.at[k], send_sem=psend.at[k],
            recv_sem=precv.at[k], device_id={"filt": other}, device_id_type=MESH,
        )

    def chip_copy(k):
        g = lax.rem(chip + k, G)
        return pltpu.make_async_remote_copy(
            src_ref=summed.at[k], dst_ref=pair.at[G + G - k], send_sem=qsend.at[k],
            recv_sem=qrecv.at[G - k], device_id={"filt": g * 2 + core}, device_id_type=MESH,
        )

    order = list(range(1, G)) + [0]
    for k in order:
        pair_copy(k).start()
    for k in order:
        g = lax.rem(chip + k, G)
        pair_copy(k).wait_recv()
        summed[k] = accb[g * 2 + core, :pixels] + pair[k]
        if k:
            chip_copy(k).start()
    forward(taps - 1)
    lanes = lax.broadcasted_iota(jnp.int32, (pixels, rows), 1)

    def closed(v):
        out = v
        for k in range(1, channels // CIB):
            out = jnp.where(lanes >= k * CIB, pltpu.roll(v, rows - k, 1), out)
        return out.astype(BF16)[:, :channels]

    conv_ref[...] = closed(gathered[:pixels])
    total = summed[0]
    for k in range(1, G):
        chip_copy(k).wait_recv()
        total = total + pair[G + G - k]
    grad_ref[...] = closed(total)

    for k in range(G):
        pair_copy(k).wait_send()
    for k in range(1, G):
        chip_copy(k).wait_send()
    for j in range(1, F):
        xcopy(j).wait_send()

    def drain(t, carry):
        @pl.when(me < D - 1)
        def _():
            for d in range(D):
                @pl.when(me - d >= 0)
                def _():
                    send(slot(t, me - d), t, me - d, 1).wait_send()

        @pl.when(me > 0)
        def _():
            for d in range(D):
                @pl.when(me + d < D)
                def _():
                    send(slot(t, me + d), t, me + d, 0).wait_send()

        return carry

    lax.fori_loop(0, taps, drain, 0)


def fast_body(D, F, inputs, filters, out_grad, block_owner):
    slots, taps = filters.shape[0], filters.shape[1]
    channels, images, pixels = inputs.shape
    tall = pixels
    rows = channels // CIB * SLAB
    pairs = slots // 2
    w = pack_filters(filters)
    x, g = inputs[:, 0].T, out_grad[:, 0].T
    idx = block_owner // slots * pairs + block_owner % pairs
    half = block_owner % slots // pairs
    G = F // 2
    vm = pl.BlockSpec(memory_space=pltpu.VMEM)
    sm = pl.BlockSpec(memory_space=pltpu.SMEM)
    dma = pltpu.SemaphoreType.DMA
    conv, grad = pl.pallas_call(
        functools.partial(main_kernel, D, F),
        out_shape=[jax.ShapeDtypeStruct((pixels, channels), BF16)] * 2,
        in_specs=[vm, vm, vm, sm, sm],
        out_specs=[vm, vm],
        scratch_shapes=[
            pltpu.VMEM((taps, D * pairs, SLAB, LANES), BF16),
            pltpu.VMEM((D * pairs, SLAB, LANES), BF16),
            pltpu.VMEM((F, tall, channels), BF16),
            pltpu.VMEM((F * rows, rows), BF16),
            pltpu.VMEM((F, tall, rows), F32),
            pltpu.VMEM((2 * G, pixels, rows), F32),
            pltpu.VMEM((tall, rows), F32),
            pltpu.VMEM((G, pixels, rows), F32),
            pltpu.VMEM((3, tall + 2 * WW, rows), F32),
            pltpu.VMEM((3, tall + 2 * WW, F * rows), F32),
            pltpu.VMEM((tall, rows), F32),
            dma((2, D, taps)), dma((D, taps)), dma((F,)), dma((F,)),
            dma((G,)), dma((G,)), dma((G + 1,)), dma((G + 1,)), dma((2,)),
        ],
        compiler_params=pltpu.CompilerParams(
            collective_id=0, has_side_effects=True, vmem_limit_bytes=60 * 1024 * 1024
        ),
    )(w, x, g, idx, half)

    return conv.T[:, None], grad.T[:, None]


def solution(mesh):
    D, F = mesh.shape["dp"], mesh.shape["filt"]
    placed = (
        P("filt", ("parts", "dp"), None),
        P(("parts", "dp"), None, None, "filt"),
        P("filt", ("parts", "dp"), None),
        P("parts"),
    )

    def body(inputs, filters, out_grad, block_owner):
        if filters.shape[0] % 2 == 0 and F % 2 == 0 and inputs.shape[1] == 1 and D <= 8:
            return fast_body(D, F, inputs, filters, out_grad, block_owner)
        return plain_body(inputs, filters, out_grad, block_owner)

    return jax.shard_map(
        body,
        mesh=mesh,
        in_specs=placed,
        out_specs=(P("filt", ("parts", "dp"), None), P("filt", ("parts", "dp"), None)),
        check_vma=False,
    )
```
